128 devices in a mesh: leaf: 64 (over y_hi, x, z, core), rhs: 2 (over y_lo).
Axes of the slice: x: 4, y: 4 (y_hi: 2, y_lo: 2; y = y_hi * 2 + y_lo), z: 4, core: 2. Of those that a mesh axis runs over, the one named last changes fastest.
Arguments:
- rhs: bfloat16 [524288, 512], P('leaf', 'rhs'), may hold values from -6 to 6
- source_basis: bfloat16 [4096, 128, 128], P('leaf', None, 'rhs'), may hold values from -0.5 to 0.5
- target_basis: bfloat16 [4096, 128, 128], P('leaf', None, 'rhs'), may hold values from -0.5 to 0.5
- near_blocks: bfloat16 [4096, 2, 128, 128], P('leaf', None, None, 'rhs'), may hold values from -0.375 to 0.375
- near_offsets: int32 [4096, 2], P('leaf'), may hold values from -2 to 2
- source_values: bfloat16 [3, 2048, 2, 2, 128, 128], P(None, 'leaf', None, None, 'rhs'), may hold values from -0.375 to 0.375
- source_scales: float32 [3, 2048, 2, 2, 128], P(None, 'leaf'), may hold values from 0.2 to 2
- target_values: bfloat16 [3, 2048, 2, 2, 128, 128], P(None, 'leaf', None, None, 'rhs'), may hold values from -0.375 to 0.375
- target_scales: float32 [3, 2048, 2, 2, 128], P(None, 'leaf'), may hold values from 0.2 to 2
Outputs:
- product: bfloat16 [524288, 512], P('leaf', 'rhs')
The draws below stay inside these ranges and needn't reach their ends.
All inputs are finite; a program needn't handle non-finite values.
Results may differ from the reference program's by a relative error of at most 0.01.
Values may be sent and summed in bfloat16 or wider, within the bound.
A program may use at most 192 MiB of HBM per device.

```python
import math
import jax
import jax.numpy as jnp
from jax import lax

M = 128
R = 128
BOX_DEV = 64
K = 2
REACH = 2
SRC_LEVELS = 3
TGT_LEVELS = 3
BOXES = 4096
ORDER = 524288
RHS = 512
N_LEAF = 64


def plant(values, rng, low, top_value):
    extent = values.shape
    spot = [jax.random.randint(jax.random.fold_in(rng, axis), (), 0, extent[axis]) for axis in range(len(extent))]
    values = values.at[tuple(spot)].set(low)
    longest = extent.index(max(extent))
    spot[longest] = (spot[longest] + 1) % extent[longest]
    return values.at[tuple(spot)].set(top_value)


def levels(stream_key, dims, shards, smallest, top_value):
    factor_of, own = 1.0, jax.random.fold_in(stream_key, 6)
    for dim, shards_of in shards:
        draws = jnp.exp(jax.random.uniform(jax.random.fold_in(own, dim), (shards_of,), jnp.float32, smallest / len(shards), top_value / len(shards)))
        factor_of = factor_of * jnp.repeat(draws, dims[dim] // shards_of).reshape([-1 if axis == dim else 1 for axis in range(len(dims))])
    return factor_of


def scatter_about(stream_key, dims, scale, limit, cuts=(), kind=jnp.bfloat16):
    result = jax.random.normal(stream_key, dims, jnp.float32) * scale
    if len(cuts) > 0:
        result = levels(stream_key, dims, cuts, -0.22, 0.18) * result
    return jnp.clip(result, min=-limit, max=limit).astype(kind)


def setup_inputs(seed: int = 0) -> dict:
    key_list = jax.random.split(jax.random.key(seed), 10)
    return {
        "rhs": scatter_about(key_list[0], (ORDER, RHS), 1.0, 6.0, ((0, 64), (1, 2))),
        "source_basis": scatter_about(key_list[1], (BOXES, M, R), M ** -0.5, 0.5, ((0, 64), (2, 2))),
        "target_basis": scatter_about(key_list[2], (BOXES, M, R), R ** -0.5, 0.5, ((0, 64), (2, 2))),
        "near_blocks": scatter_about(key_list[3], (BOXES, K, M, M), (K * M) ** -0.5, 0.375, ((0, 64), (3, 2))),
        "near_offsets": plant(jax.random.randint(key_list[4], (BOXES, K), -REACH, REACH + 1), jax.random.fold_in(key_list[4], 1), -REACH, REACH).astype(jnp.int32),
        "source_values": scatter_about(key_list[5], (SRC_LEVELS, BOXES // 2, 2, 2, R, R), (2 * R) ** -0.5, 0.375, ((1, 64), (4, 2))),
        "source_scales": jnp.clip(jnp.exp(math.log(2.0) - 2.3025851 * jax.random.uniform(key_list[6], (SRC_LEVELS, BOXES // 2, 2, 2, R), jnp.float32) ** levels(key_list[6], (SRC_LEVELS, BOXES // 2, 2, 2, R), ((1, 64),), -0.2, 0.2)), 0.2, 2.0),
        "target_values": scatter_about(key_list[7], (TGT_LEVELS, BOXES // 2, 2, 2, R, R), (2 * R) ** -0.5, 0.375, ((1, 64), (4, 2))),
        "target_scales": jnp.clip(jnp.exp(math.log(2.0) - 2.3025851 * jax.random.uniform(key_list[8], (TGT_LEVELS, BOXES // 2, 2, 2, R), jnp.float32) ** levels(key_list[8], (TGT_LEVELS, BOXES // 2, 2, 2, R), ((1, 64),), -0.2, 0.2)), 0.2, 2.0),
    }


def dequantize(values, scales):
    return (values.astype(jnp.float32) * scales[..., None, :]).astype(jnp.bfloat16)


def butterfly_level(coefficients, blocks, bit_index):
    box_total, columns, rank = coefficients.shape
    outputs = blocks.shape[-2]
    low_span = 2 ** bit_index
    high_span = box_total // (2 * low_span)
    inputs = coefficients.reshape(high_span, 2, low_span, columns, rank).astype(jnp.float32)
    matrices = blocks.reshape(high_span, low_span, 2, 2, outputs, rank).astype(jnp.float32)
    mixed = jnp.einsum("hclnr,hlocsr->holns", inputs, matrices)
    return mixed.reshape(box_total, columns, outputs).astype(jnp.bfloat16)


def reference(rhs, source_basis, target_basis, near_blocks, near_offsets, source_values, source_scales, target_values, target_scales):
    box_total = BOX_DEV * N_LEAF
    quota_boxes = BOX_DEV // N_LEAF
    columns = math.gcd(RHS, 128)
    col_groups = RHS // columns
    source_index = jnp.arange(box_total, dtype=jnp.int32)[:, None] + REACH + near_offsets.astype(jnp.int32)

    def one_group(block_rhs):
        rhs_boxes = block_rhs.reshape(box_total, M, columns)
        coefficients = jnp.einsum("bmc,bmr->bcr", rhs_boxes.astype(jnp.float32), source_basis.astype(jnp.float32)).astype(jnp.bfloat16)
        for level_index in range(SRC_LEVELS):
            coefficients = butterfly_level(coefficients, dequantize(source_values[level_index], source_scales[level_index]), level_index)
        coefficients = coefficients.reshape(N_LEAF, N_LEAF, quota_boxes, columns, R).transpose(1, 0, 2, 3, 4).reshape(box_total, columns, R)
        for level_index in range(TGT_LEVELS):
            coefficients = butterfly_level(coefficients, dequantize(target_values[level_index], target_scales[level_index]), level_index)
        far_field = jnp.einsum("bmr,bcr->bmc", target_basis.astype(jnp.float32), coefficients.astype(jnp.float32))
        padded = jnp.pad(rhs_boxes, ((REACH, REACH), (0, 0), (0, 0)))
        selected = jnp.take(padded, source_index, axis=0)
        near_field = jnp.einsum("bkmn,bknc->bmc", near_blocks.astype(jnp.float32), selected.astype(jnp.float32))
        return (far_field + near_field).astype(jnp.bfloat16).reshape(box_total * M, columns)

    grouped = rhs.reshape(box_total * M, col_groups, columns).transpose(1, 0, 2)
    results = lax.map(one_group, grouped)
    return results.transpose(1, 0, 2).reshape(box_total * M, RHS)
```

```python
import jax
import jax.numpy as jnp
from jax import lax
from jax.experimental import pallas as pl
from jax.experimental.pallas import tpu as pltpu
from jax.sharding import PartitionSpec as P

MESH = pl.DeviceIdType.MESH
LEVELS = 3
STEPS = 4
GROUP = 8
HALF = 32
ROWS = 128
COLS = 256


def dot(a, b, contract_a=1):
    return lax.dot_general(
        a, b, (((contract_a,), (0,)), ((), ())), preferred_element_type=jnp.float32
    )


def kernel(
    rhs, basis_in, basis_out, near, offsets, values_in, scales_in, values_out, scales_out,
    out,
    x, w_in, w_out, w_near, v_in, v_out, s_in, s_out, z, y, o,
    load_sem, pair_send, pair_recv, halo_send, halo_recv, mix_send, mix_recv,
    back_send, back_recv, keep_sem,
):
    leaf = lax.axis_index("leaf")
    mine = lax.axis_index("rhs")
    other = 1 - mine
    side = leaf // HALF
    slot = leaf % HALF
    turn = (leaf // GROUP) % STEPS
    partner = (leaf, other)
    low, high = leaf > 0, leaf < 2 * HALF - 1
    rows_of = pl.multiple_of(mine * 64, 64)

    def copy_to(src, dst, send, recv, device):
        return pltpu.make_async_remote_copy(
            src_ref=src, dst_ref=dst, send_sem=send, recv_sem=recv,
            device_id=device, device_id_type=MESH,
        )

    def parts(step, owner):
        g = (turn + step) % STEPS
        h = (turn + STEPS - step) % STEPS
        box, row_box = owner * HALF + GROUP * g, owner * HALF + GROUP * h
        return (
            (rhs.at[pl.ds(box, 8)], x.at[pl.ds(2 + GROUP * g, 8), mine]),
            (basis_in.at[pl.ds(box, 8)], w_in.at[pl.ds(GROUP * g, 8), pl.ds(rows_of, 64)]),
            (
                values_in.at[:, pl.ds(2 * box, 16)],
                v_in.at[:, pl.ds(2 * GROUP * g, 16), pl.ds(rows_of, 64)],
            ),
            (
                values_out.at[:, pl.ds(2 * row_box, 16)],
                v_out.at[:, pl.ds(2 * GROUP * h, 16), pl.ds(rows_of, 64)],
            ),
            (
                basis_out.at[pl.ds(row_box, 8)],
                w_out.at[pl.ds(GROUP * h, 8), pl.ds(rows_of, 64)],
            ),
            (
                near.at[pl.ds(2 * row_box, 16)],
                w_near.at[pl.ds(2 * GROUP * h, 16), pl.ds(rows_of, 64)],
            ),
        )

    def inner(owner):
        return rhs.at[pl.ds(32 - 2 * owner, 2)], x.at[pl.ds(34 - 34 * owner, 2), mine]

    def load(step, part):
        src, dst = parts(step, mine)[part]
        return pltpu.make_async_copy(src, dst, load_sem.at[6 * step + part])

    def pair(step, part):
        src, dst = parts(step, other)[part]
        at = 6 * step + part
        return copy_to(src, dst, pair_send.at[at], pair_recv.at[at], partner)

    def pair_wait(step, part):
        src, dst = parts(step, mine)[part]
        return src, dst

    load_inner = pltpu.make_async_copy(*inner(mine), load_sem.at[24])
    load_scales = (
        pltpu.make_async_copy(scales_in.at[:, pl.ds(16 * mine, 16)], s_in, load_sem.at[25]),
        pltpu.make_async_copy(scales_out.at[:, pl.ds(16 * mine, 16)], s_out, load_sem.at[26]),
    )
    pair_inner = copy_to(*inner(other), pair_send.at[24], pair_recv.at[24], partner)
    halo_up = copy_to(
        rhs.at[pl.ds(62, 2)], x.at[pl.ds(0, 2), mine],
        halo_send.at[0], halo_recv.at[mine], (leaf + 1, 0),
    )
    halo_down = copy_to(
        rhs.at[pl.ds(0, 2)], x.at[pl.ds(34, 2), mine],
        halo_send.at[1], halo_recv.at[mine], (leaf - 1, 1),
    )

    def mix(j):
        return copy_to(
            z.at[j], y.at[slot], mix_send.at[j], mix_recv.at[slot], (mine * HALF + j, side)
        )

    def is_self(j):
        return (mine * HALF + j == leaf) & (side == mine)

    def back(b):
        return copy_to(
            o.at[other, b], out.at[mine * HALF + b], back_send.at[b], back_recv.at[b], partner
        )

    def keep(b):
        return pltpu.make_async_copy(o.at[mine, b], out.at[mine * HALF + b], keep_sem.at[b])

    for copy in load_scales:
        copy.start()
    for step in range(STEPS):
        for part in range(3):
            load(step, part).start()

    barrier = pltpu.get_barrier_semaphore()

    def greet(*device):
        pl.semaphore_signal(barrier, inc=1, device_id=device, device_id_type=MESH)

    greet(leaf, other)

    @pl.loop(0, HALF)
    def _(j):
        @pl.when(jnp.logical_not(is_self(j)))
        def _():
            greet(mine * HALF + j, side)

    @pl.when((mine == 0) & low)
    def _():
        greet(leaf - 1, 0)
        greet(leaf - 1, 1)

    @pl.when((mine == 1) & high)
    def _():
        greet(leaf + 1, 0)
        greet(leaf + 1, 1)

    pl.semaphore_wait(
        barrier,
        1 + HALF - (side == mine).astype(jnp.int32)
        + low.astype(jnp.int32) + high.astype(jnp.int32),
    )

    for step in range(STEPS):
        for part in range(3):
            pair(step, part).start()
    pair_inner.start()

    @pl.when(high)
    def _():
        halo_up.start()

    @pl.when(low)
    def _():
        halo_down.start()

    for step in range(STEPS):
        for part in range(3, 6):
            pair(step, part).start()
    for step in range(STEPS):
        for part in range(3, 6):
            load(step, part).start()
    load_inner.start()

    @pl.when((mine == 0) & jnp.logical_not(low))
    def _():
        x[0:2] = jnp.zeros((2, 2, ROWS, COLS), jnp.bfloat16)

    @pl.when((mine == 1) & jnp.logical_not(high))
    def _():
        x[34:36] = jnp.zeros((2, 2, ROWS, COLS), jnp.bfloat16)

    def arrived(step, part):
        load(step, part).wait()
        src, dst = parts(step, other)[part]
        at = 6 * step + part
        into = parts(step, mine)[part][1]
        copy_to(src, into, pair_send.at[at], pair_recv.at[at], partner).wait_recv()

    def levels(coeff, blocks, scales, g):
        for t in range(LEVELS):
            @pl.loop(0, 4)
            def _(q):
                i = GROUP * g + (q // 2**t) * 2 ** (t + 1) + q % 2**t
                j = i + 2**t
                pair_at = 4 * g + q

                def block(at_o, at_c):
                    return (
                        blocks[t, 4 * pair_at + 2 * at_o + at_c].astype(jnp.float32)
                        * scales[t, pair_at, at_o, at_c:at_c + 1, :]
                    ).astype(jnp.bfloat16)

                both = jnp.concatenate([coeff[i], coeff[j]], axis=0)
                first = dot(jnp.concatenate([block(0, 0), block(0, 1)], axis=1), both)
                second = dot(jnp.concatenate([block(1, 0), block(1, 1)], axis=1), both)
                coeff[i] = first.astype(jnp.bfloat16)
                coeff[j] = second.astype(jnp.bfloat16)

    for copy in load_scales:
        copy.wait()

    @pl.loop(0, STEPS)
    def _(step):
        g = (turn + step) % STEPS
        for part in range(3):
            arrived(step, part)

        @pl.loop(0, GROUP)
        def _(i):
            b = GROUP * g + i
            for c in range(2):
                z[b, :, COLS * c:COLS * (c + 1)] = dot(w_in[b], x[2 + b, c]).astype(jnp.bfloat16)

        levels(z, v_in, s_in, g)

        @pl.loop(0, GROUP)
        def _(i):
            j = GROUP * g + i

            @pl.when(is_self(j))
            def _():
                y[slot] = z[j]

            @pl.when(jnp.logical_not(is_self(j)))
            def _():
                mix(j).start()

    load_inner.wait()
    copy_to(
        inner(mine)[0], x.at[pl.ds(34 - 34 * mine, 2), other],
        pair_send.at[24], pair_recv.at[24], partner,
    ).wait_recv()

    @pl.when(((mine == 0) & low) | ((mine == 1) & high))
    def _():
        for c in range(2):
            copy_to(
                rhs.at[pl.ds(0, 2)], x.at[pl.ds(34 * mine, 2), c],
                halo_send.at[0], halo_recv.at[c], partner,
            ).wait_recv()

    @pl.loop(0, STEPS)
    def _(step):
        h = (turn + STEPS - step) % STEPS
        for part in range(3, 6):
            arrived(step, part)

        @pl.loop(0, GROUP)
        def _(i):
            d = GROUP * h + i

            @pl.when(jnp.logical_not(is_self(d)))
            def _():
                copy_to(
                    z.at[d], y.at[d], mix_send.at[d], mix_recv.at[d], partner
                ).wait_recv()

        levels(y, v_out, s_out, h)

        @pl.loop(0, GROUP)
        def _(i):
            b = GROUP * h + i
            first = b + 2 + offsets[0, HALF * mine + b]
            second = b + 2 + offsets[1, HALF * mine + b]
            left = jnp.concatenate([w_out[b], w_near[2 * b], w_near[2 * b + 1]], axis=0)
            for c in range(2):
                right = jnp.concatenate(
                    [y[b, :, COLS * c:COLS * (c + 1)], x[first, c], x[second, c]], axis=0
                )
                o[c, b] = dot(left, right, 0).astype(jnp.bfloat16)
            back(b).start()
            keep(b).start()

    for step in range(STEPS):
        for part in range(6):
            pair(step, part).wait_send()
    pair_inner.wait_send()

    @pl.when(high)
    def _():
        halo_up.wait_send()

    @pl.when(low)
    def _():
        halo_down.wait_send()

    @pl.loop(0, HALF)
    def _(j):
        @pl.when(jnp.logical_not(is_self(j)))
        def _():
            mix(j).wait_send()

        keep(j).wait()
        back(j).wait_send()
        copy_to(
            o.at[other, j], out.at[other * HALF + j], back_send.at[j], back_recv.at[j], partner
        ).wait_recv()


def on_device(
    rhs, source_basis, target_basis, near_blocks, near_offsets,
    source_values, source_scales, target_values, target_scales,
):
    boxes = source_basis.shape[0]
    anywhere = pl.BlockSpec(memory_space=pl.ANY)
    bf16, f32 = jnp.bfloat16, jnp.float32
    product = pl.pallas_call(
        kernel,
        out_shape=jax.ShapeDtypeStruct((boxes, ROWS, COLS), bf16),
        in_specs=[anywhere] * 4 + [pl.BlockSpec(memory_space=pltpu.SMEM)] + [anywhere] * 4,
        out_specs=anywhere,
        scratch_shapes=[
            pltpu.VMEM((HALF + 4, 2, ROWS, COLS), bf16),
            pltpu.VMEM((HALF, 128, 128), bf16),
            pltpu.VMEM((HALF, 128, 128), bf16),
            pltpu.VMEM((2 * HALF, 128, 128), bf16),
            pltpu.VMEM((LEVELS, 2 * HALF, 128, 128), bf16),
            pltpu.VMEM((LEVELS, 2 * HALF, 128, 128), bf16),
            pltpu.VMEM((LEVELS, HALF // 2, 2, 2, 128), f32),
            pltpu.VMEM((LEVELS, HALF // 2, 2, 2, 128), f32),
            pltpu.VMEM((HALF, 128, 2 * COLS), bf16),
            pltpu.VMEM((HALF, 128, 2 * COLS), bf16),
            pltpu.VMEM((2, HALF, ROWS, COLS), bf16),
            pltpu.SemaphoreType.DMA((27,)),
            pltpu.SemaphoreType.DMA((25,)),
            pltpu.SemaphoreType.DMA((25,)),
            pltpu.SemaphoreType.DMA((2,)),
            pltpu.SemaphoreType.DMA((2,)),
            pltpu.SemaphoreType.DMA((HALF,)),
            pltpu.SemaphoreType.DMA((HALF,)),
            pltpu.SemaphoreType.DMA((HALF,)),
            pltpu.SemaphoreType.DMA((HALF,)),
            pltpu.SemaphoreType.DMA((HALF,)),
        ],
        compiler_params=pltpu.CompilerParams(
            collective_id=0, has_side_effects=True, vmem_limit_bytes=56 << 20
        ),
        name="butterfly",
    )(
        rhs.reshape(boxes, ROWS, COLS),
        jnp.swapaxes(source_basis, 1, 2),
        jnp.swapaxes(target_basis, 1, 2),
        jnp.swapaxes(near_blocks, 2, 3).reshape(2 * boxes, 64, 128),
        near_offsets.T,
        source_values.reshape(LEVELS, 2 * boxes, 64, 128),
        source_scales,
        target_values.reshape(LEVELS, 2 * boxes, 64, 128),
        target_scales,
    )
    return product.reshape(boxes * ROWS, COLS)


def solution(mesh):
    placed = (
        P("leaf", "rhs"),
        P("leaf", None, "rhs"),
        P("leaf", None, "rhs"),
        P("leaf", None, None, "rhs"),
        P("leaf", None),
        P(None, "leaf", None, None, "rhs", None),
        P(None, "leaf", None, None, None),
        P(None, "leaf", None, None, "rhs", None),
        P(None, "leaf", None, None, None),
    )
    return jax.shard_map(
        on_device, mesh=mesh, in_specs=placed, out_specs=P("leaf", "rhs"), check_vma=False
    )
```

```python
import jax
import jax.numpy as jnp
from jax import lax
from jax.experimental import pallas as pl
from jax.experimental.pallas import tpu as pltpu
from jax.sharding import PartitionSpec as P

MESH = pl.DeviceIdType.MESH
LEVELS = 3
STEPS = 4
GROUP = 8
HALF = 32
ROWS = 128
COLS = 256


def dot(a, b, contract_a=1):
    return lax.dot_general(
        a, b, (((contract_a,), (0,)), ((), ())), preferred_element_type=jnp.float32
    )


def kernel(
    rhs, basis_in, basis_out, near, offsets, values_in, scales_in, values_out, scales_out,
    out,
    x, x_other, w_in, w_out, w_near, w_edge, v_in, v_out, s_in, s_out, z, y, o, edge,
    load_sem, pair_send, pair_recv, halo_send, halo_recv, mix_send, mix_recv,
    back_send, back_recv, known,
):
    leaf = lax.axis_index("leaf")
    mine = lax.axis_index("rhs")
    other = 1 - mine
    side = leaf // HALF
    slot = leaf % HALF
    turn = (leaf // GROUP) % STEPS
    partner = (leaf, other)
    low, high = leaf > 0, leaf < 2 * HALF - 1
    half_rows = pl.ds(pl.multiple_of(mine * 64, 64), 64)
    place = (2 * side + mine, slot // 8, slot // 2 % 4, slot % 2)

    def around(axis, by):
        spot = list(place)
        spot[axis] = (spot[axis] + by) % (2 if axis == 3 else 4)
        return (
            (spot[0] // 2) * HALF + spot[1] * 8 + spot[2] * 2 + spot[3], spot[0] % 2
        )

    def signal(sem, device):
        pl.semaphore_signal(sem, inc=1, device_id=device, device_id_type=MESH)

    def copy_to(src, dst, send, recv, device):
        return pltpu.make_async_remote_copy(
            src_ref=src, dst_ref=dst, send_sem=send, recv_sem=recv,
            device_id=device, device_id_type=MESH,
        )

    def parts(step, owner, columns):
        g = (turn + step) % STEPS
        h = (turn + STEPS - step) % STEPS
        box, row_box = owner * HALF + GROUP * g, owner * HALF + GROUP * h
        return (
            (rhs.at[pl.ds(box, 8)], columns(box, GROUP * g)),
            (basis_in.at[pl.ds(box, 8)], w_in.at[pl.ds(GROUP * g, 8), half_rows]),
            (
                values_in.at[:, pl.ds(2 * box, 16)],
                v_in.at[:, pl.ds(2 * GROUP * g, 16), half_rows],
            ),
            (
                values_out.at[:, pl.ds(2 * row_box, 16)],
                v_out.at[:, pl.ds(2 * GROUP * h, 16), half_rows],
            ),
            (basis_out.at[pl.ds(row_box, 8)], w_out.at[pl.ds(GROUP * h, 8), half_rows]),
            (
                near.at[pl.ds(2 * row_box, 16)],
                w_near.at[pl.ds(2 * GROUP * h, 16), half_rows],
            ),
        )

    def load(step, part):
        src, dst = parts(step, mine, lambda box, at: x.at[pl.ds(2 + box, 8)])[part]
        return pltpu.make_async_copy(src, dst, load_sem.at[6 * step + part])

    def pair(step, part, owner=other):
        src, dst = parts(step, owner, lambda box, at: x_other.at[pl.ds(at, 8)])[part]
        at = 6 * step + part
        return copy_to(src, dst, pair_send.at[at], pair_recv.at[at], partner)

    def edges(at, owner):
        first = 2 * (HALF * owner + 30 * at)
        return near.at[pl.ds(first, 4)], w_edge.at[pl.ds(4 * at, 4), half_rows]

    load_rest = [
        pltpu.make_async_copy(*edges(at, other), load_sem.at[24 + at]) for at in range(2)
    ] + [
        pltpu.make_async_copy(
            rhs.at[pl.ds(HALF * other, HALF)], x.at[pl.ds(2 + HALF * other, HALF)],
            load_sem.at[26],
        )
    ]
    load_scales = [
        pltpu.make_async_copy(scales_in.at[:, pl.ds(16 * mine, 16)], s_in, load_sem.at[27]),
        pltpu.make_async_copy(scales_out.at[:, pl.ds(16 * mine, 16)], s_out, load_sem.at[28]),
    ]
    pair_edges = [
        copy_to(*edges(at, mine), pair_send.at[24 + at], pair_recv.at[24 + at], partner)
        for at in range(2)
    ]
    halo_up = copy_to(
        rhs.at[pl.ds(62, 2)], x.at[pl.ds(0, 2)],
        halo_send.at[0], halo_recv.at[0], (leaf + 1, mine),
    )
    halo_down = copy_to(
        rhs.at[pl.ds(0, 2)], x.at[pl.ds(66, 2)],
        halo_send.at[1], halo_recv.at[1], (leaf - 1, mine),
    )

    def mix(j):
        return copy_to(
            z.at[j], y.at[slot], mix_send.at[j], mix_recv.at[slot], (mine * HALF + j, side)
        )

    def is_self(j):
        return (mine * HALF + j == leaf) & (side == mine)

    def on_edge(b):
        return (b < 2) | (b >= HALF - 2)

    def back(b, owner=mine):
        return copy_to(
            o.at[b], out.at[owner * HALF + b], back_send.at[b], back_recv.at[b], partner
        )

    def back_edge(b):
        return copy_to(
            o.at[b], edge.at[b % 28], back_send.at[b], back_recv.at[b], partner
        )

    barrier = pltpu.get_barrier_semaphore()
    beside = [around(axis, by) for axis in range(3) for by in (1, 3)] + [around(3, 1)]
    for device in beside:
        signal(barrier, device)
    for step in range(STEPS):
        for part in range(3):
            load(step, part).start()
    for copy in load_scales:
        copy.start()
    pl.semaphore_wait(barrier, len(beside))

    for step in range(STEPS):
        for part in range(3):
            pair(step, part).start()
    for step in range(STEPS):
        for part in range(3, 6):
            pair(step, part).start()
    for copy in pair_edges:
        copy.start()

    spread = ((1, (1,)), (2, (1, 3)), (2, (1,)), (3, (1,)), (0, (1, 3)), (0, (1,)))
    for stage, (axis, hops) in enumerate(spread):
        for by in hops:
            signal(known.at[stage], around(axis, by))
        pl.semaphore_wait(known.at[stage], len(hops))

    @pl.when(high)
    def _():
        halo_up.start()

    @pl.when(low)
    def _():
        halo_down.start()

    for step in range(STEPS):
        for part in range(3, 6):
            load(step, part).start()
    for copy in load_rest:
        copy.start()

    @pl.when(jnp.logical_not(low))
    def _():
        x[0:2] = jnp.zeros((2, ROWS, COLS), jnp.bfloat16)

    @pl.when(jnp.logical_not(high))
    def _():
        x[66:68] = jnp.zeros((2, ROWS, COLS), jnp.bfloat16)

    def arrived(step, part):
        load(step, part).wait()
        pair(step, part, mine).wait_recv()

    def levels(coeff, blocks, scales, g):
        for t in range(LEVELS):
            @pl.loop(0, 4)
            def _(q):
                i = GROUP * g + (q // 2**t) * 2 ** (t + 1) + q % 2**t
                j = i + 2**t
                pair_at = 4 * g + q

                def block(at_o, at_c):
                    return (
                        blocks[t, 4 * pair_at + 2 * at_o + at_c].astype(jnp.float32)
                        * scales[t, pair_at, at_o, at_c:at_c + 1, :]
                    ).astype(jnp.bfloat16)

                above = jnp.concatenate([block(0, 0), block(0, 1)], axis=1)
                below = jnp.concatenate([block(1, 0), block(1, 1)], axis=1)
                for c in range(2):
                    both = jnp.concatenate([coeff[i, c], coeff[j, c]], axis=0)
                    first, second = dot(above, both), dot(below, both)
                    coeff[i, c] = first.astype(jnp.bfloat16)
                    coeff[j, c] = second.astype(jnp.bfloat16)

    for copy in load_scales:
        copy.wait()

    @pl.loop(0, STEPS)
    def _(step):
        g = (turn + step) % STEPS
        for part in range(3):
            arrived(step, part)

        @pl.loop(0, GROUP)
        def _(i):
            b = GROUP * g + i
            z[b, mine] = dot(w_in[b], x[2 + HALF * mine + b]).astype(jnp.bfloat16)
            z[b, other] = dot(w_in[b], x_other[b]).astype(jnp.bfloat16)

        levels(z, v_in, s_in, g)

        @pl.loop(0, GROUP)
        def _(i):
            j = GROUP * g + i

            @pl.when(is_self(j))
            def _():
                y[slot] = z[j]

            @pl.when(jnp.logical_not(is_self(j)))
            def _():
                mix(j).start()

    for copy in load_rest:
        copy.wait()

    @pl.when(low)
    def _():
        halo_up.wait_recv()

    @pl.when(high)
    def _():
        halo_down.wait_recv()

    @pl.loop(0, STEPS)
    def _(step):
        h = (turn + STEPS - step) % STEPS
        for part in range(3, 6):
            arrived(step, part)

        @pl.loop(0, GROUP)
        def _(i):
            d = GROUP * h + i

            @pl.when(jnp.logical_not(is_self(d)))
            def _():
                copy_to(
                    z.at[d], y.at[d], mix_send.at[d], mix_recv.at[d], partner
                ).wait_recv()

        levels(y, v_out, s_out, h)

        @pl.loop(0, GROUP)
        def _(i):
            b = GROUP * h + (i + 6) % GROUP
            row = HALF * mine + b
            first, second = offsets[0, row], offsets[1, row]

            @pl.when(on_edge(b))
            def _():
                o[b] = dot(w_out[b], y[b, other], 0).astype(jnp.bfloat16)
                back_edge(b).start()

            left = jnp.concatenate([w_out[b], w_near[2 * b], w_near[2 * b + 1]], axis=0)

            @pl.when(jnp.logical_not(on_edge(b)))
            def _():
                right = jnp.concatenate(
                    [y[b, other], x_other[b + first], x_other[b + second]], axis=0
                )
                o[b] = dot(left, right, 0).astype(jnp.bfloat16)
                back(b).start()

            right = jnp.concatenate(
                [y[b, mine], x[2 + row + first], x[2 + row + second]], axis=0
            )
            out[row] = dot(left, right, 0).astype(jnp.bfloat16)

    for copy in pair_edges:
        copy.wait_recv()

    @pl.loop(0, 4)
    def _(e):
        b = e + 28 * (e // 2)
        row = HALF * other + b
        left = jnp.concatenate([w_edge[2 * e], w_edge[2 * e + 1]], axis=0)
        right = jnp.concatenate(
            [x[2 + row + offsets[0, row]], x[2 + row + offsets[1, row]]], axis=0
        )
        add = dot(left, right, 0)
        back_edge(b).wait_recv()
        out[row] = (edge[e].astype(jnp.float32) + add).astype(jnp.bfloat16)

    for step in range(STEPS):
        for part in range(6):
            pair(step, part).wait_send()
    for copy in pair_edges:
        copy.wait_send()

    @pl.when(high)
    def _():
        halo_up.wait_send()

    @pl.when(low)
    def _():
        halo_down.wait_send()

    @pl.loop(0, HALF)
    def _(j):
        @pl.when(jnp.logical_not(is_self(j)))
        def _():
            mix(j).wait_send()

        back(j).wait_send()

        @pl.when(jnp.logical_not(on_edge(j)))
        def _():
            back(j, other).wait_recv()


def on_device(
    rhs, source_basis, target_basis, near_blocks, near_offsets,
    source_values, source_scales, target_values, target_scales,
):
    boxes = source_basis.shape[0]
    anywhere = pl.BlockSpec(memory_space=pltpu.HBM)
    bf16, f32 = jnp.bfloat16, jnp.float32
    product = pl.pallas_call(
        kernel,
        out_shape=pltpu.VMEM((boxes, ROWS, COLS), bf16),
        in_specs=[anywhere] * 4 + [pl.BlockSpec(memory_space=pltpu.SMEM)] + [anywhere] * 4,
        out_specs=pl.BlockSpec(memory_space=pltpu.VMEM),
        scratch_shapes=[
            pltpu.VMEM((2 * HALF + 4, ROWS, COLS), bf16),
            pltpu.VMEM((HALF, ROWS, COLS), bf16),
            pltpu.VMEM((HALF, 128, 128), bf16),
            pltpu.VMEM((HALF, 128, 128), bf16),
            pltpu.VMEM((2 * HALF, 128, 128), bf16),
            pltpu.VMEM((8, 128, 128), bf16),
            pltpu.VMEM((LEVELS, 2 * HALF, 128, 128), bf16),
            pltpu.VMEM((LEVELS, 2 * HALF, 128, 128), bf16),
            pltpu.VMEM((LEVELS, HALF // 2, 2, 2, 128), f32),
            pltpu.VMEM((LEVELS, HALF // 2, 2, 2, 128), f32),
            pltpu.VMEM((HALF, 2, 128, COLS), bf16),
            pltpu.VMEM((HALF, 2, 128, COLS), bf16),
            pltpu.VMEM((HALF, ROWS, COLS), bf16),
            pltpu.VMEM((4, ROWS, COLS), bf16),
            pltpu.SemaphoreType.DMA((29,)),
            pltpu.SemaphoreType.DMA((26,)),
            pltpu.SemaphoreType.DMA((26,)),
            pltpu.SemaphoreType.DMA((2,)),
            pltpu.SemaphoreType.DMA((2,)),
            pltpu.SemaphoreType.DMA((HALF,)),
            pltpu.SemaphoreType.DMA((HALF,)),
            pltpu.SemaphoreType.DMA((HALF,)),
            pltpu.SemaphoreType.DMA((HALF,)),
            pltpu.SemaphoreType.REGULAR((6,)),
        ],
        compiler_params=pltpu.CompilerParams(
            collective_id=0, has_side_effects=True, vmem_limit_bytes=58 << 20
        ),
        name="butterfly",
    )(
        rhs.reshape(boxes, ROWS, COLS),
        jnp.swapaxes(source_basis, 1, 2),
        jnp.swapaxes(target_basis, 1, 2),
        jnp.swapaxes(near_blocks, 2, 3).reshape(2 * boxes, 64, 128),
        near_offsets.T,
        source_values.reshape(LEVELS, 2 * boxes, 64, 128),
        source_scales,
        target_values.reshape(LEVELS, 2 * boxes, 64, 128),
        target_scales,
    )
    return product.reshape(boxes * ROWS, COLS)


def solution(mesh):
    placed = (
        P("leaf", "rhs"),
        P("leaf", None, "rhs"),
        P("leaf", None, "rhs"),
        P("leaf", None, None, "rhs"),
        P("leaf", None),
        P(None, "leaf", None, None, "rhs", None),
        P(None, "leaf", None, None, None),
        P(None, "leaf", None, None, "rhs", None),
        P(None, "leaf", None, None, None),
    )
    return jax.shard_map(
        on_device, mesh=mesh, in_specs=placed, out_specs=P("leaf", "rhs"), check_vma=False
    )
```

```python
import jax
import jax.numpy as jnp
from jax import lax
from jax.experimental import pallas as pl
from jax.experimental.pallas import tpu as pltpu
from jax.sharding import PartitionSpec as P

MESH = pl.DeviceIdType.MESH
LEVELS = 3
STEPS = 4
GROUP = 8
HALF = 32
ROWS = 128
COLS = 256


def dot(a, b, contract_a=1):
    return lax.dot_general(
        a, b, (((contract_a,), (0,)), ((), ())), preferred_element_type=jnp.float32
    )


def kernel(
    rhs, basis_in, basis_out, near, near_offsets, values_in, scales_in, values_out, scales_out,
    out,
    x, x_other, w_in, w_out, w_near, w_edge, v_in, v_out, s_in, s_out, z, y, o, edge, offsets,
    load_sem, pair_send, pair_recv, halo_send, halo_recv, mix_send, mix_recv,
    back_send, back_recv, known,
):
    leaf = lax.axis_index("leaf")
    mine = lax.axis_index("rhs")
    other = 1 - mine
    side = leaf // HALF
    slot = leaf % HALF
    turn = (leaf // GROUP) % STEPS
    partner = (leaf, other)
    low, high = leaf > 0, leaf < 2 * HALF - 1
    half_rows = pl.ds(pl.multiple_of(mine * 64, 64), 64)
    place = (2 * side + mine, slot // 8, slot // 2 % 4, slot % 2)

    def around(axis, by):
        spot = list(place)
        spot[axis] = (spot[axis] + by) % (2 if axis == 3 else 4)
        return (
            (spot[0] // 2) * HALF + spot[1] * 8 + spot[2] * 2 + spot[3], spot[0] % 2
        )

    def signal(sem, device):
        pl.semaphore_signal(sem, inc=1, device_id=device, device_id_type=MESH)

    def copy_to(src, dst, send, recv, device):
        return pltpu.make_async_remote_copy(
            src_ref=src, dst_ref=dst, send_sem=send, recv_sem=recv,
            device_id=device, device_id_type=MESH,
        )

    def parts(step, owner, columns):
        g = (turn + step) % STEPS
        h = (turn + STEPS - step) % STEPS
        box, row_box = owner * HALF + GROUP * g, owner * HALF + GROUP * h
        return (
            (rhs.at[pl.ds(box, 8)], columns(box, GROUP * g)),
            (basis_in.at[pl.ds(box, 8)], w_in.at[pl.ds(GROUP * g, 8), half_rows]),
            (
                values_in.at[:, pl.ds(2 * box, 16)],
                v_in.at[:, pl.ds(2 * GROUP * g, 16), half_rows],
            ),
            (
                values_out.at[:, pl.ds(2 * row_box, 16)],
                v_out.at[:, pl.ds(2 * GROUP * h, 16), half_rows],
            ),
            (basis_out.at[pl.ds(row_box, 8)], w_out.at[pl.ds(GROUP * h, 8), half_rows]),
            (
                near.at[pl.ds(2 * row_box, 16)],
                w_near.at[pl.ds(2 * GROUP * h, 16), half_rows],
            ),
        )

    def load(step, part):
        src, dst = parts(step, mine, lambda box, at: x.at[pl.ds(2 + box, 8)])[part]
        return pltpu.make_async_copy(src, dst, load_sem.at[6 * step + part])

    def pair(step, part, owner=other):
        src, dst = parts(step, owner, lambda box, at: x_other.at[pl.ds(at, 8)])[part]
        at = 6 * step + part
        return copy_to(src, dst, pair_send.at[at], pair_recv.at[at], partner)

    def edges(at, owner):
        first = 2 * (HALF * owner + 30 * at)
        return near.at[pl.ds(first, 4)], w_edge.at[pl.ds(4 * at, 4), half_rows]

    load_rest = [
        pltpu.make_async_copy(*edges(at, other), load_sem.at[24 + at]) for at in range(2)
    ] + [
        pltpu.make_async_copy(
            rhs.at[pl.ds(HALF * other, HALF)], x.at[pl.ds(2 + HALF * other, HALF)],
            load_sem.at[26],
        )
    ]
    load_scales = [
        pltpu.make_async_copy(scales_in.at[:, pl.ds(16 * mine, 16)], s_in, load_sem.at[27]),
        pltpu.make_async_copy(scales_out.at[:, pl.ds(16 * mine, 16)], s_out, load_sem.at[28]),
        pltpu.make_async_copy(near_offsets, offsets, load_sem.at[29]),
    ]
    pair_edges = [
        copy_to(*edges(at, mine), pair_send.at[24 + at], pair_recv.at[24 + at], partner)
        for at in range(2)
    ]
    halo_up = copy_to(
        rhs.at[pl.ds(62, 2)], x.at[pl.ds(0, 2)],
        halo_send.at[0], halo_recv.at[0], (leaf + 1, mine),
    )
    halo_down = copy_to(
        rhs.at[pl.ds(0, 2)], x.at[pl.ds(66, 2)],
        halo_send.at[1], halo_recv.at[1], (leaf - 1, mine),
    )

    def mix(j):
        return copy_to(
            z.at[j], y.at[slot], mix_send.at[j], mix_recv.at[slot], (mine * HALF + j, side)
        )

    def is_self(j):
        return (mine * HALF + j == leaf) & (side == mine)

    def on_edge(b):
        return (b < 2) | (b >= HALF - 2)

    def back(b, owner=mine):
        return copy_to(
            o.at[b], out.at[owner * HALF + b], back_send.at[b], back_recv.at[b], partner
        )

    def back_edge(b):
        return copy_to(
            o.at[b], edge.at[b % 28], back_send.at[b], back_recv.at[b], partner
        )

    barrier = pltpu.get_barrier_semaphore()
    core = place[3]
    hub = (mine == 0) & (core == 0)
    beside_hub = (mine == 1) & (core == 0)
    lead = (mine == 0) & (core == 1)

    @pl.when(jnp.logical_not(beside_hub))
    def _():
        signal(barrier, partner)

    @pl.when(jnp.logical_not(hub))
    def _():
        pl.semaphore_wait(barrier, 1)

    @pl.when(beside_hub)
    def _():
        signal(known.at[0], partner)

    @pl.when(hub)
    def _():
        pl.semaphore_wait(known.at[0], 1)

    for step in range(STEPS):
        for part in range(3):
            pair(step, part).start()
    for step in range(STEPS):
        for part in range(3, 6):
            pair(step, part).start()
    for copy in pair_edges:
        copy.start()
    for step in range(STEPS):
        for part in range(3):
            load(step, part).start()
    for copy in load_scales:
        copy.start()
    for step in range(STEPS):
        for part in range(3, 6):
            load(step, part).start()
    for copy in load_rest:
        copy.start()

    @pl.when(lead)
    def _():
        signal(barrier, around(3, 1))
        pl.semaphore_wait(known.at[6], 1)
        signal(known.at[7], partner)

    @pl.when(hub)
    def _():
        sides = [around(axis, by) for axis in (1, 2) for by in (1, 3)] + [around(0, 2)]
        for device in sides:
            signal(barrier, device)
        pl.semaphore_wait(barrier, len(sides) + 1)
        spread = ((1, (1, 3)), (1, (1,)), (2, (1, 3)), (2, (1,)), (0, (2,)))
        for stage, (axis, hops) in enumerate(spread):
            for by in hops:
                signal(known.at[1 + stage], around(axis, by))
            pl.semaphore_wait(known.at[1 + stage], len(hops))
        signal(known.at[6], around(3, 1))
        signal(known.at[7], partner)

    @pl.when(mine == 1)
    def _():
        pl.semaphore_wait(known.at[7], 1)

    @pl.when(high)
    def _():
        halo_up.start()

    @pl.when(low)
    def _():
        halo_down.start()

    @pl.when(jnp.logical_not(low))
    def _():
        x[0:2] = jnp.zeros((2, ROWS, COLS), jnp.bfloat16)

    @pl.when(jnp.logical_not(high))
    def _():
        x[66:68] = jnp.zeros((2, ROWS, COLS), jnp.bfloat16)

    def arrived(step, part):
        load(step, part).wait()
        pair(step, part, mine).wait_recv()

    def levels(coeff, blocks, scales, g):
        for t in range(LEVELS):
            @pl.loop(0, 4)
            def _(q):
                i = GROUP * g + (q // 2**t) * 2 ** (t + 1) + q % 2**t
                j = i + 2**t
                pair_at = 4 * g + q

                def block(at_o, at_c):
                    return (
                        blocks[t, 4 * pair_at + 2 * at_o + at_c].astype(jnp.float32)
                        * scales[t, pair_at, at_o, at_c:at_c + 1, :]
                    ).astype(jnp.bfloat16)

                above = jnp.concatenate([block(0, 0), block(0, 1)], axis=1)
                below = jnp.concatenate([block(1, 0), block(1, 1)], axis=1)
                for c in range(2):
                    both = jnp.concatenate([coeff[i, c], coeff[j, c]], axis=0)
                    first, second = dot(above, both), dot(below, both)
                    coeff[i, c] = first.astype(jnp.bfloat16)
                    coeff[j, c] = second.astype(jnp.bfloat16)

    for copy in load_scales:
        copy.wait()

    @pl.loop(0, STEPS)
    def _(step):
        g = (turn + step) % STEPS
        for part in range(3):
            arrived(step, part)

        @pl.loop(0, GROUP)
        def _(i):
            b = GROUP * g + i
            z[b, mine] = dot(w_in[b], x[2 + HALF * mine + b]).astype(jnp.bfloat16)
            z[b, other] = dot(w_in[b], x_other[b]).astype(jnp.bfloat16)

        levels(z, v_in, s_in, g)

        @pl.loop(0, GROUP)
        def _(i):
            j = GROUP * g + i

            @pl.when(is_self(j))
            def _():
                y[slot] = z[j]

            @pl.when(jnp.logical_not(is_self(j)))
            def _():
                mix(j).start()

    for copy in load_rest:
        copy.wait()

    @pl.when(low)
    def _():
        halo_up.wait_recv()

    @pl.when(high)
    def _():
        halo_down.wait_recv()

    @pl.loop(0, STEPS)
    def _(step):
        h = (turn + STEPS - step) % STEPS
        for part in range(3, 6):
            arrived(step, part)

        @pl.loop(0, GROUP)
        def _(i):
            d = GROUP * h + i

            @pl.when(jnp.logical_not(is_self(d)))
            def _():
                copy_to(
                    z.at[d], y.at[d], mix_send.at[d], mix_recv.at[d], partner
                ).wait_recv()

        levels(y, v_out, s_out, h)

        @pl.loop(0, GROUP)
        def _(i):
            b = GROUP * h + (i + 6) % GROUP
            row = HALF * mine + b
            first, second = offsets[0, row], offsets[1, row]

            @pl.when(on_edge(b))
            def _():
                o[b] = dot(w_out[b], y[b, other], 0).astype(jnp.bfloat16)
                back_edge(b).start()

            left = jnp.concatenate([w_out[b], w_near[2 * b], w_near[2 * b + 1]], axis=0)

            @pl.when(jnp.logical_not(on_edge(b)))
            def _():
                right = jnp.concatenate(
                    [y[b, other], x_other[b + first], x_other[b + second]], axis=0
                )
                o[b] = dot(left, right, 0).astype(jnp.bfloat16)
                back(b).start()

            right = jnp.concatenate(
                [y[b, mine], x[2 + row + first], x[2 + row + second]], axis=0
            )
            out[row] = dot(left, right, 0).astype(jnp.bfloat16)

    for copy in pair_edges:
        copy.wait_recv()

    @pl.loop(0, 4)
    def _(e):
        b = e + 28 * (e // 2)
        row = HALF * other + b
        left = jnp.concatenate([w_edge[2 * e], w_edge[2 * e + 1]], axis=0)
        right = jnp.concatenate(
            [x[2 + row + offsets[0, row]], x[2 + row + offsets[1, row]]], axis=0
        )
        add = dot(left, right, 0)
        back_edge(b).wait_recv()
        out[row] = (edge[e].astype(jnp.float32) + add).astype(jnp.bfloat16)

    for step in range(STEPS):
        for part in range(6):
            pair(step, part).wait_send()
    for copy in pair_edges:
        copy.wait_send()

    @pl.when(high)
    def _():
        halo_up.wait_send()

    @pl.when(low)
    def _():
        halo_down.wait_send()

    @pl.loop(0, HALF)
    def _(j):
        @pl.when(jnp.logical_not(is_self(j)))
        def _():
            mix(j).wait_send()

        back(j).wait_send()

        @pl.when(jnp.logical_not(on_edge(j)))
        def _():
            back(j, other).wait_recv()


def on_device(
    rhs, source_basis, target_basis, near_blocks, near_offsets,
    source_values, source_scales, target_values, target_scales,
):
    boxes = source_basis.shape[0]
    anywhere = pl.BlockSpec(memory_space=pltpu.HBM)
    bf16, f32 = jnp.bfloat16, jnp.float32
    product = pl.pallas_call(
        kernel,
        out_shape=pltpu.VMEM((boxes, ROWS, COLS), bf16),
        in_specs=[anywhere] * 9,
        out_specs=pl.BlockSpec(memory_space=pltpu.VMEM),
        scratch_shapes=[
            pltpu.VMEM((2 * HALF + 4, ROWS, COLS), bf16),
            pltpu.VMEM((HALF, ROWS, COLS), bf16),
            pltpu.VMEM((HALF, 128, 128), bf16),
            pltpu.VMEM((HALF, 128, 128), bf16),
            pltpu.VMEM((2 * HALF, 128, 128), bf16),
            pltpu.VMEM((8, 128, 128), bf16),
            pltpu.VMEM((LEVELS, 2 * HALF, 128, 128), bf16),
            pltpu.VMEM((LEVELS, 2 * HALF, 128, 128), bf16),
            pltpu.VMEM((LEVELS, HALF // 2, 2, 2, 128), f32),
            pltpu.VMEM((LEVELS, HALF // 2, 2, 2, 128), f32),
            pltpu.VMEM((HALF, 2, 128, COLS), bf16),
            pltpu.VMEM((HALF, 2, 128, COLS), bf16),
            pltpu.VMEM((HALF, ROWS, COLS), bf16),
            pltpu.VMEM((4, ROWS, COLS), bf16),
            pltpu.SMEM((2, 2 * HALF), jnp.int32),
            pltpu.SemaphoreType.DMA((30,)),
            pltpu.SemaphoreType.DMA((26,)),
            pltpu.SemaphoreType.DMA((26,)),
            pltpu.SemaphoreType.DMA((2,)),
            pltpu.SemaphoreType.DMA((2,)),
            pltpu.SemaphoreType.DMA((HALF,)),
            pltpu.SemaphoreType.DMA((HALF,)),
            pltpu.SemaphoreType.DMA((HALF,)),
            pltpu.SemaphoreType.DMA((HALF,)),
            pltpu.SemaphoreType.REGULAR((8,)),
        ],
        compiler_params=pltpu.CompilerParams(
            collective_id=0, has_side_effects=True, vmem_limit_bytes=58 << 20
        ),
        name="butterfly",
    )(
        rhs.reshape(boxes, ROWS, COLS),
        jnp.swapaxes(source_basis, 1, 2),
        jnp.swapaxes(target_basis, 1, 2),
        jnp.swapaxes(near_blocks, 2, 3).reshape(2 * boxes, 64, 128),
        near_offsets.T,
        source_values.reshape(LEVELS, 2 * boxes, 64, 128),
        source_scales,
        target_values.reshape(LEVELS, 2 * boxes, 64, 128),
        target_scales,
    )
    return product.reshape(boxes * ROWS, COLS)


def solution(mesh):
    placed = (
        P("leaf", "rhs"),
        P("leaf", None, "rhs"),
        P("leaf", None, "rhs"),
        P("leaf", None, None, "rhs"),
        P("leaf", None),
        P(None, "leaf", None, None, "rhs", None),
        P(None, "leaf", None, None, None),
        P(None, "leaf", None, None, "rhs", None),
        P(None, "leaf", None, None, None),
    )
    return jax.shard_map(
        on_device, mesh=mesh, in_specs=placed, out_specs=P("leaf", "rhs"), check_vma=False
    )
```

```python
import jax
import jax.numpy as jnp
from jax import lax
from jax.experimental import pallas as pl
from jax.experimental.pallas import tpu as pltpu
from jax.sharding import PartitionSpec as P

MESH = pl.DeviceIdType.MESH
LEVELS = 3
STEPS = 4
GROUP = 8
HALF = 32
ROWS = 128
COLS = 256


def dot(a, b, contract_a=1):
    return lax.dot_general(
        a, b, (((contract_a,), (0,)), ((), ())), preferred_element_type=jnp.float32
    )


def kernel(
    rhs, basis_in, basis_out, near, near_offsets, values_in, scales_in, values_out, scales_out,
    out,
    x, x_other, w_in, w_out, w_near, w_edge, v_in, v_out, s_in, s_out, z, y, o, edge, offsets,
    load_sem, pair_send, pair_recv, halo_send, halo_recv, mix_send, mix_recv,
    back_send, back_recv, known, hop, hop_sem,
):
    leaf = lax.axis_index("leaf")
    mine = lax.axis_index("rhs")
    other = 1 - mine
    side = leaf // HALF
    slot = leaf % HALF
    turn = (leaf // GROUP) % STEPS
    partner = (leaf, other)
    low, high = leaf > 0, leaf < 2 * HALF - 1
    half_rows = pl.ds(pl.multiple_of(mine * 64, 64), 64)
    place = (2 * side + mine, slot // 8, slot // 2 % 4, slot % 2)

    def around(axis, by):
        spot = list(place)
        spot[axis] = (spot[axis] + by) % (2 if axis == 3 else 4)
        return (
            (spot[0] // 2) * HALF + spot[1] * 8 + spot[2] * 2 + spot[3], spot[0] % 2
        )

    def signal(sem, device):
        pl.semaphore_signal(sem, inc=1, device_id=device, device_id_type=MESH)

    def copy_to(src, dst, send, recv, device):
        return pltpu.make_async_remote_copy(
            src_ref=src, dst_ref=dst, send_sem=send, recv_sem=recv,
            device_id=device, device_id_type=MESH,
        )

    def parts(step, owner):
        g = (turn + step) % STEPS
        h = (turn + STEPS - step) % STEPS
        box, row_box = owner * HALF + GROUP * g, owner * HALF + GROUP * h
        return (
            (rhs.at[pl.ds(box, 8)], x_other.at[pl.ds(GROUP * g, 8)]),
            (basis_in.at[pl.ds(box, 8)], w_in.at[pl.ds(GROUP * g, 8), half_rows]),
            (
                values_in.at[:, pl.ds(2 * box, 16)],
                v_in.at[:, pl.ds(2 * GROUP * g, 16), half_rows],
            ),
            (
                values_out.at[:, pl.ds(2 * row_box, 16)],
                v_out.at[:, pl.ds(2 * GROUP * h, 16), half_rows],
            ),
            (basis_out.at[pl.ds(row_box, 8)], w_out.at[pl.ds(GROUP * h, 8), half_rows]),
            (
                near.at[pl.ds(2 * row_box, 16)],
                w_near.at[pl.ds(2 * GROUP * h, 16), half_rows],
            ),
        )

    def pair(step, part):
        src, dst = parts(step, other)[part]
        recv = pair_recv.at[step + STEPS * (part // 3)]
        return copy_to(src, dst, pair_send.at[part], recv, partner)

    def halves(box):
        return (
            (basis_in.at[pl.ds(box, HALF)], w_in.at[:, half_rows]),
            (values_in.at[:, pl.ds(2 * box, 2 * HALF)], v_in.at[:, :, half_rows]),
            (values_out.at[:, pl.ds(2 * box, 2 * HALF)], v_out.at[:, :, half_rows]),
            (basis_out.at[pl.ds(box, HALF)], w_out.at[:, half_rows]),
            (near.at[pl.ds(2 * box, 2 * HALF)], w_near.at[:, half_rows]),
        )

    def bulk(boxes, recv):
        return copy_to(
            rhs.at[pl.ds(0, boxes)], x_other.at[pl.ds(0, boxes)], pair_send.at[0], recv, partner
        )

    def edges(at, owner):
        first = 2 * (HALF * owner + 30 * at)
        return near.at[pl.ds(first, 4)], w_edge.at[pl.ds(4 * at, 4), half_rows]

    loads = [
        pltpu.make_async_copy(src, dst, load_sem.at[n])
        for n, (src, dst) in enumerate(
            ((rhs, x.at[pl.ds(2, 2 * HALF)]),)
            + halves(HALF * mine)
            + (edges(0, other), edges(1, other))
            + (
                (scales_in.at[:, pl.ds(16 * mine, 16)], s_in),
                (scales_out.at[:, pl.ds(16 * mine, 16)], s_out),
                (near_offsets, offsets),
            )
        )
    ]
    pair_edges = [
        copy_to(*edges(at, mine), pair_send.at[6], pair_recv.at[8], partner)
        for at in range(2)
    ]
    halo_up = copy_to(
        rhs.at[pl.ds(62, 2)], x.at[pl.ds(0, 2)],
        halo_send.at[0], halo_recv.at[0], (leaf + 1, mine),
    )
    halo_down = copy_to(
        rhs.at[pl.ds(0, 2)], x.at[pl.ds(66, 2)],
        halo_send.at[1], halo_recv.at[1], (leaf - 1, mine),
    )

    seam_up, seam_down = leaf == HALF - 1, leaf == HALF

    def seam_first(n):
        rows = pl.ds(32 * n, 32)
        up = copy_to(
            rhs.at[pl.ds(62, 2), rows], hop, halo_send.at[0], hop_sem.at[0],
            (leaf - 6 + 2 * n, mine),
        )
        down = copy_to(
            rhs.at[pl.ds(0, 2), rows], hop, halo_send.at[1], hop_sem.at[0],
            (leaf + 2 * n, mine),
        )
        return up, down

    def seam_last(n, src_up, src_down, send_up, send_down):
        rows = pl.ds(32 * n, 32)
        up = copy_to(
            src_up, x.at[pl.ds(0, 2), rows], send_up, halo_recv.at[0], (HALF, mine)
        )
        down = copy_to(
            src_down, x.at[pl.ds(66, 2), rows], send_down, halo_recv.at[1], (HALF - 1, mine)
        )
        return up, down

    def seam_direct(n):
        rows = pl.ds(32 * n, 32)
        return seam_last(
            n, rhs.at[pl.ds(62, 2), rows], rhs.at[pl.ds(0, 2), rows],
            halo_send.at[0], halo_send.at[1],
        )

    def seam_relay(n):
        return seam_last(n, hop, hop, hop_sem.at[1], hop_sem.at[1])

    def mix(j):
        return copy_to(
            z.at[j], y.at[slot], mix_send.at[0], mix_recv.at[slot // GROUP],
            (mine * HALF + j, side),
        )

    def mixed(boxes, recv):
        return copy_to(
            z.at[pl.ds(0, boxes)], y.at[pl.ds(0, boxes)], mix_send.at[0], recv, partner
        )

    def is_self(j):
        return (mine * HALF + j == leaf) & (side == mine)

    def on_edge(b):
        return (b < 2) | (b >= HALF - 2)

    def back(b):
        return copy_to(
            o.at[b], out.at[mine * HALF + b], back_send.at[0], back_recv.at[0], partner
        )

    def back_edge(b):
        return copy_to(
            o.at[b], edge.at[b % 28], back_send.at[0], back_recv.at[1], partner
        )

    barrier = pltpu.get_barrier_semaphore()
    core = place[3]
    hub = (mine == 0) & (core == 0)
    beside_hub = (mine == 1) & (core == 0)
    lead = (mine == 0) & (core == 1)

    @pl.when(jnp.logical_not(beside_hub))
    def _():
        signal(barrier, partner)

    @pl.when(jnp.logical_not(hub))
    def _():
        pl.semaphore_wait(barrier, 1)

    @pl.when(beside_hub)
    def _():
        signal(known.at[0], partner)

    @pl.when(hub)
    def _():
        pl.semaphore_wait(known.at[0], 1)

    for step in range(STEPS):
        for part in range(3):
            pair(step, part).start()
    for step in range(STEPS):
        for part in range(3, 6):
            pair(step, part).start()
    for copy in pair_edges:
        copy.start()
    for copy in loads:
        copy.start()

    @pl.when(lead)
    def _():
        signal(barrier, around(3, 1))
        pl.semaphore_wait(known.at[6], 1)
        signal(known.at[7], partner)

    @pl.when(hub)
    def _():
        sides = [around(axis, by) for axis in (1, 2) for by in (1, 3)] + [around(0, 2)]
        for device in sides:
            signal(barrier, device)
        pl.semaphore_wait(barrier, len(sides) + 1)
        spread = ((1, (1, 3)), (1, (1,)), (2, (1, 3)), (2, (1,)), (0, (2,)))
        for stage, (axis, hops) in enumerate(spread):
            for by in hops:
                signal(known.at[1 + stage], around(axis, by))
            pl.semaphore_wait(known.at[1 + stage], len(hops))
        signal(known.at[6], around(3, 1))
        signal(known.at[7], partner)

    @pl.when(mine == 1)
    def _():
        pl.semaphore_wait(known.at[7], 1)

    @pl.when(high & jnp.logical_not(seam_up))
    def _():
        halo_up.start()

    @pl.when(low & jnp.logical_not(seam_down))
    def _():
        halo_down.start()

    @pl.when(seam_up)
    def _():
        for n in range(3):
            seam_first(n)[0].start()
        seam_direct(3)[0].start()

    @pl.when(seam_down)
    def _():
        for n in range(1, 4):
            seam_first(n)[1].start()
        seam_direct(0)[1].start()

    for n in range(3):
        @pl.when(leaf == HALF - 7 + 2 * n)
        def _():
            seam_first(n)[0].wait_recv()
            seam_relay(n)[0].start()

    for n in range(1, 4):
        @pl.when(leaf == HALF + 2 * n)
        def _():
            seam_first(n)[1].wait_recv()
            seam_relay(n)[1].start()

    @pl.when(jnp.logical_not(low))
    def _():
        x[0:2] = jnp.zeros((2, ROWS, COLS), jnp.bfloat16)

    @pl.when(jnp.logical_not(high))
    def _():
        x[66:68] = jnp.zeros((2, ROWS, COLS), jnp.bfloat16)

    def levels(coeff, blocks, scales, g):
        for t in range(LEVELS):
            @pl.loop(0, 4)
            def _(q):
                i = GROUP * g + (q // 2**t) * 2 ** (t + 1) + q % 2**t
                j = i + 2**t
                pair_at = 4 * g + q

                def block(at_o, at_c):
                    return (
                        blocks[t, 4 * pair_at + 2 * at_o + at_c].astype(jnp.float32)
                        * scales[t, pair_at, at_o, at_c:at_c + 1, :]
                    ).astype(jnp.bfloat16)

                above = jnp.concatenate([block(0, 0), block(0, 1)], axis=1)
                below = jnp.concatenate([block(1, 0), block(1, 1)], axis=1)
                for c in range(2):
                    both = jnp.concatenate([coeff[i, c], coeff[j, c]], axis=0)
                    first, second = dot(above, both), dot(below, both)
                    coeff[i, c] = first.astype(jnp.bfloat16)
                    coeff[j, c] = second.astype(jnp.bfloat16)

    for copy in loads:
        copy.wait()

    @pl.loop(0, STEPS)
    def _(step):
        g = (turn + step) % STEPS
        bulk(22, pair_recv.at[step]).wait_recv()

        @pl.loop(0, GROUP)
        def _(i):
            b = GROUP * g + i
            z[b, mine] = dot(w_in[b], x[2 + HALF * mine + b]).astype(jnp.bfloat16)
            z[b, other] = dot(w_in[b], x_other[b]).astype(jnp.bfloat16)

        levels(z, v_in, s_in, g)

        @pl.loop(0, GROUP)
        def _(i):
            j = GROUP * g + i

            @pl.when(is_self(j))
            def _():
                y[slot] = z[j]

            @pl.when(jnp.logical_not(is_self(j)))
            def _():
                mix(j).start()

    @pl.when(low)
    def _():
        halo_up.wait_recv()

    @pl.when(high)
    def _():
        halo_down.wait_recv()

    @pl.loop(0, STEPS)
    def _(step):
        h = (turn + STEPS - step) % STEPS
        bulk(18, pair_recv.at[STEPS + step]).wait_recv()
        with_self = (side == mine) & (slot // GROUP == h)

        @pl.when(with_self)
        def _():
            mixed(GROUP - 1, mix_recv.at[h]).wait_recv()

        @pl.when(jnp.logical_not(with_self))
        def _():
            mixed(GROUP, mix_recv.at[h]).wait_recv()

        levels(y, v_out, s_out, h)

        @pl.loop(0, GROUP)
        def _(i):
            b = GROUP * h + (i + 6) % GROUP
            row = HALF * mine + b
            first, second = offsets[0, row], offsets[1, row]

            @pl.when(on_edge(b))
            def _():
                o[b] = dot(w_out[b], y[b, other], 0).astype(jnp.bfloat16)
                back_edge(b).start()

            left = jnp.concatenate([w_out[b], w_near[2 * b], w_near[2 * b + 1]], axis=0)

            @pl.when(jnp.logical_not(on_edge(b)))
            def _():
                right = jnp.concatenate(
                    [y[b, other], x_other[b + first], x_other[b + second]], axis=0
                )
                o[b] = dot(left, right, 0).astype(jnp.bfloat16)
                back(b).start()

            right = jnp.concatenate(
                [y[b, mine], x[2 + row + first], x[2 + row + second]], axis=0
            )
            out[row] = dot(left, right, 0).astype(jnp.bfloat16)

    bulk(HALF, pair_recv.at[0]).wait_send()
    for n, (src, dst) in enumerate(halves(0)):
        copy_to(src, dst, pair_send.at[1 + n], pair_recv.at[0], partner).wait_send()
    pair_edge = copy_to(
        near.at[pl.ds(0, 8)], w_edge.at[:, half_rows], pair_send.at[6], pair_recv.at[8], partner
    )
    pair_edge.wait_send()

    @pl.when(high)
    def _():
        halo_up.wait_send()

    @pl.when(low)
    def _():
        halo_down.wait_send()

    for n in range(3):
        @pl.when((leaf == HALF - 7 + 2 * n) | (leaf == HALF + 2 * n + 2))
        def _():
            seam_relay(n)[0].wait_send()

    @pl.when(side == mine)
    def _():
        mixed(HALF - 1, mix_recv.at[0]).wait_send()

    @pl.when(side != mine)
    def _():
        mixed(HALF, mix_recv.at[0]).wait_send()

    pair_edge.wait_recv()
    copy_to(
        o.at[pl.ds(0, 4)], edge, back_send.at[0], back_recv.at[1], partner
    ).wait_recv()

    @pl.loop(0, 4)
    def _(e):
        row = HALF * other + e + 28 * (e // 2)
        left = jnp.concatenate([w_edge[2 * e], w_edge[2 * e + 1]], axis=0)
        right = jnp.concatenate(
            [x[2 + row + offsets[0, row]], x[2 + row + offsets[1, row]]], axis=0
        )
        out[row] = (edge[e].astype(jnp.float32) + dot(left, right, 0)).astype(jnp.bfloat16)

    copy_to(
        o, out.at[pl.ds(0, HALF)], back_send.at[0], back_recv.at[0], partner
    ).wait_send()
    copy_to(
        o.at[pl.ds(0, 28)], out.at[pl.ds(0, 28)], back_send.at[0], back_recv.at[0], partner
    ).wait_recv()


def on_device(
    rhs, source_basis, target_basis, near_blocks, near_offsets,
    source_values, source_scales, target_values, target_scales,
):
    boxes = source_basis.shape[0]
    anywhere = pl.BlockSpec(memory_space=pltpu.HBM)
    bf16, f32 = jnp.bfloat16, jnp.float32
    product = pl.pallas_call(
        kernel,
        out_shape=pltpu.VMEM((boxes, ROWS, COLS), bf16),
        in_specs=[anywhere] * 9,
        out_specs=pl.BlockSpec(memory_space=pltpu.VMEM),
        scratch_shapes=[
            pltpu.VMEM((2 * HALF + 4, ROWS, COLS), bf16),
            pltpu.VMEM((HALF, ROWS, COLS), bf16),
            pltpu.VMEM((HALF, 128, 128), bf16),
            pltpu.VMEM((HALF, 128, 128), bf16),
            pltpu.VMEM((2 * HALF, 128, 128), bf16),
            pltpu.VMEM((8, 128, 128), bf16),
            pltpu.VMEM((LEVELS, 2 * HALF, 128, 128), bf16),
            pltpu.VMEM((LEVELS, 2 * HALF, 128, 128), bf16),
            pltpu.VMEM((LEVELS, HALF // 2, 2, 2, 128), f32),
            pltpu.VMEM((LEVELS, HALF // 2, 2, 2, 128), f32),
            pltpu.VMEM((HALF, 2, 128, COLS), bf16),
            pltpu.VMEM((HALF, 2, 128, COLS), bf16),
            pltpu.VMEM((HALF, ROWS, COLS), bf16),
            pltpu.VMEM((4, ROWS, COLS), bf16),
            pltpu.SMEM((2, 2 * HALF), jnp.int32),
            pltpu.SemaphoreType.DMA((11,)),
            pltpu.SemaphoreType.DMA((7,)),
            pltpu.SemaphoreType.DMA((9,)),
            pltpu.SemaphoreType.DMA((2,)),
            pltpu.SemaphoreType.DMA((2,)),
            pltpu.SemaphoreType.DMA((1,)),
            pltpu.SemaphoreType.DMA((STEPS,)),
            pltpu.SemaphoreType.DMA((1,)),
            pltpu.SemaphoreType.DMA((2,)),
            pltpu.SemaphoreType.REGULAR((8,)),
            pltpu.VMEM((2, 32, COLS), bf16),
            pltpu.SemaphoreType.DMA((2,)),
        ],
        compiler_params=pltpu.CompilerParams(
            collective_id=0, has_side_effects=True, vmem_limit_bytes=58 << 20
        ),
        name="butterfly",
    )(
        rhs.reshape(boxes, ROWS, COLS),
        jnp.swapaxes(source_basis, 1, 2),
        jnp.swapaxes(target_basis, 1, 2),
        jnp.swapaxes(near_blocks, 2, 3).reshape(2 * boxes, 64, 128),
        near_offsets.T,
        source_values.reshape(LEVELS, 2 * boxes, 64, 128),
        source_scales,
        target_values.reshape(LEVELS, 2 * boxes, 64, 128),
        target_scales,
    )
    return product.reshape(boxes * ROWS, COLS)


def solution(mesh):
    placed = (
        P("leaf", "rhs"),
        P("leaf", None, "rhs"),
        P("leaf", None, "rhs"),
        P("leaf", None, None, "rhs"),
        P("leaf", None),
        P(None, "leaf", None, None, "rhs", None),
        P(None, "leaf", None, None, None),
        P(None, "leaf", None, None, "rhs", None),
        P(None, "leaf", None, None, None),
    )
    return jax.shard_map(
        on_device, mesh=mesh, in_specs=placed, out_specs=P("leaf", "rhs"), check_vma=False
    )
```

```python
import jax
import jax.numpy as jnp
from jax import lax
from jax.experimental import pallas as pl
from jax.experimental.pallas import tpu as pltpu
from jax.sharding import PartitionSpec as P

MESH = pl.DeviceIdType.MESH
LEVELS = 3
STEPS = 4
GROUP = 8
HALF = 32
ROWS = 128
COLS = 256


def dot(a, b, contract_a=1):
    return lax.dot_general(
        a, b, (((contract_a,), (0,)), ((), ())), preferred_element_type=jnp.float32
    )


def kernel(
    rhs, basis_in, basis_out, near, near_offsets, values_in, scales_in, values_out, scales_out,
    out,
    x, x_other, w_in, w_out, w_near, w_edge, v_in, v_out, s_in, s_out, z, y, o, edge, offsets,
    load_sem, pair_send, pair_recv, halo_send, halo_recv, mix_send, mix_recv,
    back_send, back_recv, known, hop, hop_sem,
):
    leaf = lax.axis_index("leaf")
    mine = lax.axis_index("rhs")
    other = 1 - mine
    side = leaf // HALF
    slot = leaf % HALF
    turn = (leaf // GROUP) % STEPS
    partner = (leaf, other)
    low, high = leaf > 0, leaf < 2 * HALF - 1
    half_rows = pl.ds(pl.multiple_of(mine * 64, 64), 64)
    place = (2 * side + mine, slot // 8, slot // 2 % 4, slot % 2)

    def around(axis, by):
        spot = list(place)
        spot[axis] = (spot[axis] + by) % (2 if axis == 3 else 4)
        return (
            (spot[0] // 2) * HALF + spot[1] * 8 + spot[2] * 2 + spot[3], spot[0] % 2
        )

    def signal(sem, device):
        pl.semaphore_signal(sem, inc=1, device_id=device, device_id_type=MESH)

    def copy_to(src, dst, send, recv, device):
        return pltpu.make_async_remote_copy(
            src_ref=src, dst_ref=dst, send_sem=send, recv_sem=recv,
            device_id=device, device_id_type=MESH,
        )

    def parts(step, owner):
        g = (turn + step) % STEPS
        h = (turn + STEPS - step) % STEPS
        box, row_box = owner * HALF + GROUP * g, owner * HALF + GROUP * h
        return (
            (rhs.at[pl.ds(box, 8)], x_other.at[pl.ds(GROUP * g, 8)]),
            (basis_in.at[pl.ds(box, 8)], w_in.at[pl.ds(GROUP * g, 8), half_rows]),
            (
                values_in.at[:, pl.ds(2 * box, 16)],
                v_in.at[:, pl.ds(2 * GROUP * g, 16), half_rows],
            ),
            (
                values_out.at[:, pl.ds(2 * row_box, 16)],
                v_out.at[:, pl.ds(2 * GROUP * h, 16), half_rows],
            ),
            (basis_out.at[pl.ds(row_box, 8)], w_out.at[pl.ds(GROUP * h, 8), half_rows]),
            (
                near.at[pl.ds(2 * row_box, 16)],
                w_near.at[pl.ds(2 * GROUP * h, 16), half_rows],
            ),
        )

    def pair(step, part):
        src, dst = parts(step, other)[part]
        recv = pair_recv.at[step + STEPS * (part // 3)]
        return copy_to(src, dst, pair_send.at[part], recv, partner)

    def start_pair(step, part):
        src, dst = parts(step, other)[part]
        recv = pair_recv.at[step + STEPS * (part // 3)]
        if part in (2, 3):
            cuts = [(t, pl.ds(4 * n, 4)) for t in range(LEVELS) for n in range(4)]
        else:
            size = {0: 1, 1: 4, 4: 4, 5: 4}[part]
            cuts = [(pl.ds(size * n, size),) for n in range(src.shape[0] // size)]
        for at in cuts:
            copy_to(src.at[at], dst.at[at], pair_send.at[part], recv, partner).start()

    def halves(box):
        return (
            (basis_in.at[pl.ds(box, HALF)], w_in.at[:, half_rows]),
            (values_in.at[:, pl.ds(2 * box, 2 * HALF)], v_in.at[:, :, half_rows]),
            (values_out.at[:, pl.ds(2 * box, 2 * HALF)], v_out.at[:, :, half_rows]),
            (basis_out.at[pl.ds(box, HALF)], w_out.at[:, half_rows]),
            (near.at[pl.ds(2 * box, 2 * HALF)], w_near.at[:, half_rows]),
        )

    def bulk(boxes, recv):
        return copy_to(
            rhs.at[pl.ds(0, boxes)], x_other.at[pl.ds(0, boxes)], pair_send.at[0], recv, partner
        )

    def edges(at, owner):
        first = 2 * (HALF * owner + 30 * at)
        return near.at[pl.ds(first, 4)], w_edge.at[pl.ds(4 * at, 4), half_rows]

    loads = [
        pltpu.make_async_copy(src, dst, load_sem.at[n])
        for n, (src, dst) in enumerate(
            ((rhs, x.at[pl.ds(2, 2 * HALF)]),)
            + halves(HALF * mine)
            + (edges(0, other), edges(1, other))
            + (
                (scales_in.at[:, pl.ds(16 * mine, 16)], s_in),
                (scales_out.at[:, pl.ds(16 * mine, 16)], s_out),
                (near_offsets, offsets),
            )
        )
    ]
    pair_edges = [
        copy_to(*edges(at, mine), pair_send.at[6], pair_recv.at[8], partner)
        for at in range(2)
    ]
    halo_up = copy_to(
        rhs.at[pl.ds(62, 2)], x.at[pl.ds(0, 2)],
        halo_send.at[0], halo_recv.at[0], (leaf + 1, mine),
    )
    halo_down = copy_to(
        rhs.at[pl.ds(0, 2)], x.at[pl.ds(66, 2)],
        halo_send.at[1], halo_recv.at[1], (leaf - 1, mine),
    )

    seam_up, seam_down = leaf == HALF - 1, leaf == HALF

    def seam_first(n):
        rows = pl.ds(32 * n, 32)
        up = copy_to(
            rhs.at[pl.ds(62, 2), rows], hop, halo_send.at[0], hop_sem.at[0],
            (leaf - 6 + 2 * n, mine),
        )
        down = copy_to(
            rhs.at[pl.ds(0, 2), rows], hop, halo_send.at[1], hop_sem.at[0],
            (leaf + 2 * n, mine),
        )
        return up, down

    def seam_last(n, src_up, src_down, send_up, send_down):
        rows = pl.ds(32 * n, 32)
        up = copy_to(
            src_up, x.at[pl.ds(0, 2), rows], send_up, halo_recv.at[0], (HALF, mine)
        )
        down = copy_to(
            src_down, x.at[pl.ds(66, 2), rows], send_down, halo_recv.at[1], (HALF - 1, mine)
        )
        return up, down

    def seam_direct(n):
        rows = pl.ds(32 * n, 32)
        return seam_last(
            n, rhs.at[pl.ds(62, 2), rows], rhs.at[pl.ds(0, 2), rows],
            halo_send.at[0], halo_send.at[1],
        )

    def seam_relay(n):
        return seam_last(n, hop, hop, hop_sem.at[1], hop_sem.at[1])

    def mix(j):
        return copy_to(
            z.at[j], y.at[slot], mix_send.at[0], mix_recv.at[slot // GROUP],
            (mine * HALF + j, side),
        )

    def mixed(boxes, recv):
        return copy_to(
            z.at[pl.ds(0, boxes)], y.at[pl.ds(0, boxes)], mix_send.at[0], recv, partner
        )

    def is_self(j):
        return (mine * HALF + j == leaf) & (side == mine)

    def on_edge(b):
        return (b < 2) | (b >= HALF - 2)

    def back(b):
        return copy_to(
            o.at[b], out.at[mine * HALF + b], back_send.at[0], back_recv.at[0], partner
        )

    def back_edge(b):
        return copy_to(
            o.at[b], edge.at[b % 28], back_send.at[0], back_recv.at[1], partner
        )

    barrier = pltpu.get_barrier_semaphore()
    core = place[3]
    hub = (mine == 0) & (core == 0)
    beside_hub = (mine == 1) & (core == 0)
    lead = (mine == 0) & (core == 1)

    @pl.when(jnp.logical_not(beside_hub))
    def _():
        signal(barrier, partner)

    @pl.when(jnp.logical_not(hub))
    def _():
        pl.semaphore_wait(barrier, 1)

    @pl.when(beside_hub)
    def _():
        signal(known.at[0], partner)

    @pl.when(hub)
    def _():
        pl.semaphore_wait(known.at[0], 1)

    for step in range(STEPS):
        for part in range(3):
            start_pair(step, part)
    for step in range(STEPS):
        for part in range(3, 6):
            start_pair(step, part)
    for copy in pair_edges:
        copy.start()
    for copy in loads:
        copy.start()

    @pl.when(lead)
    def _():
        signal(barrier, around(3, 1))
        pl.semaphore_wait(known.at[6], 1)
        signal(known.at[7], partner)

    @pl.when(hub)
    def _():
        sides = [around(axis, by) for axis in (1, 2) for by in (1, 3)] + [around(0, 2)]
        for device in sides:
            signal(barrier, device)
        pl.semaphore_wait(barrier, len(sides) + 1)
        spread = ((1, (1, 3)), (1, (1,)), (2, (1, 3)), (2, (1,)), (0, (2,)))
        for stage, (axis, hops) in enumerate(spread):
            for by in hops:
                signal(known.at[1 + stage], around(axis, by))
            pl.semaphore_wait(known.at[1 + stage], len(hops))
        signal(known.at[6], around(3, 1))
        signal(known.at[7], partner)

    @pl.when(mine == 1)
    def _():
        pl.semaphore_wait(known.at[7], 1)

    @pl.when(high & jnp.logical_not(seam_up))
    def _():
        halo_up.start()

    @pl.when(low & jnp.logical_not(seam_down))
    def _():
        halo_down.start()

    @pl.when(seam_up)
    def _():
        for n in range(3):
            seam_first(n)[0].start()
        seam_direct(3)[0].start()

    @pl.when(seam_down)
    def _():
        for n in range(1, 4):
            seam_first(n)[1].start()
        seam_direct(0)[1].start()

    for n in range(3):
        @pl.when(leaf == HALF - 7 + 2 * n)
        def _():
            seam_first(n)[0].wait_recv()
            seam_relay(n)[0].start()

    for n in range(1, 4):
        @pl.when(leaf == HALF + 2 * n)
        def _():
            seam_first(n)[1].wait_recv()
            seam_relay(n)[1].start()

    @pl.when(jnp.logical_not(low))
    def _():
        x[0:2] = jnp.zeros((2, ROWS, COLS), jnp.bfloat16)

    @pl.when(jnp.logical_not(high))
    def _():
        x[66:68] = jnp.zeros((2, ROWS, COLS), jnp.bfloat16)

    def levels(coeff, blocks, scales, g):
        for t in range(LEVELS):
            @pl.loop(0, 4)
            def _(q):
                i = GROUP * g + (q // 2**t) * 2 ** (t + 1) + q % 2**t
                j = i + 2**t
                pair_at = 4 * g + q

                def block(at_o, at_c):
                    return (
                        blocks[t, 4 * pair_at + 2 * at_o + at_c].astype(jnp.float32)
                        * scales[t, pair_at, at_o, at_c:at_c + 1, :]
                    ).astype(jnp.bfloat16)

                above = jnp.concatenate([block(0, 0), block(0, 1)], axis=1)
                below = jnp.concatenate([block(1, 0), block(1, 1)], axis=1)
                for c in range(2):
                    both = jnp.concatenate([coeff[i, c], coeff[j, c]], axis=0)
                    first, second = dot(above, both), dot(below, both)
                    coeff[i, c] = first.astype(jnp.bfloat16)
                    coeff[j, c] = second.astype(jnp.bfloat16)

    for copy in loads:
        copy.wait()

    @pl.loop(0, STEPS)
    def _(step):
        g = (turn + step) % STEPS
        bulk(22, pair_recv.at[step]).wait_recv()

        @pl.loop(0, GROUP)
        def _(i):
            b = GROUP * g + i
            z[b, mine] = dot(w_in[b], x[2 + HALF * mine + b]).astype(jnp.bfloat16)
            z[b, other] = dot(w_in[b], x_other[b]).astype(jnp.bfloat16)

        levels(z, v_in, s_in, g)

        @pl.loop(0, GROUP)
        def _(i):
            j = GROUP * g + i

            @pl.when(is_self(j))
            def _():
                y[slot] = z[j]

            @pl.when(jnp.logical_not(is_self(j)))
            def _():
                mix(j).start()

    @pl.when(low)
    def _():
        halo_up.wait_recv()

    @pl.when(high)
    def _():
        halo_down.wait_recv()

    @pl.loop(0, STEPS)
    def _(step):
        h = (turn + STEPS - step) % STEPS
        bulk(18, pair_recv.at[STEPS + step]).wait_recv()
        with_self = (side == mine) & (slot // GROUP == h)

        @pl.when(with_self)
        def _():
            mixed(GROUP - 1, mix_recv.at[h]).wait_recv()

        @pl.when(jnp.logical_not(with_self))
        def _():
            mixed(GROUP, mix_recv.at[h]).wait_recv()

        levels(y, v_out, s_out, h)

        @pl.loop(0, GROUP)
        def _(i):
            b = GROUP * h + (i + 6) % GROUP
            row = HALF * mine + b
            first, second = offsets[0, row], offsets[1, row]

            @pl.when(on_edge(b))
            def _():
                o[b] = dot(w_out[b], y[b, other], 0).astype(jnp.bfloat16)
                back_edge(b).start()

            left = jnp.concatenate([w_out[b], w_near[2 * b], w_near[2 * b + 1]], axis=0)

            @pl.when(jnp.logical_not(on_edge(b)))
            def _():
                right = jnp.concatenate(
                    [y[b, other], x_other[b + first], x_other[b + second]], axis=0
                )
                o[b] = dot(left, right, 0).astype(jnp.bfloat16)
                back(b).start()

            right = jnp.concatenate(
                [y[b, mine], x[2 + row + first], x[2 + row + second]], axis=0
            )
            out[row] = dot(left, right, 0).astype(jnp.bfloat16)

    bulk(HALF, pair_recv.at[0]).wait_send()
    for n, (src, dst) in enumerate(halves(0)):
        copy_to(src, dst, pair_send.at[1 + n], pair_recv.at[0], partner).wait_send()
    pair_edge = copy_to(
        near.at[pl.ds(0, 8)], w_edge.at[:, half_rows], pair_send.at[6], pair_recv.at[8], partner
    )
    pair_edge.wait_send()

    @pl.when(high)
    def _():
        halo_up.wait_send()

    @pl.when(low)
    def _():
        halo_down.wait_send()

    for n in range(3):
        @pl.when((leaf == HALF - 7 + 2 * n) | (leaf == HALF + 2 * n + 2))
        def _():
            seam_relay(n)[0].wait_send()

    @pl.when(side == mine)
    def _():
        mixed(HALF - 1, mix_recv.at[0]).wait_send()

    @pl.when(side != mine)
    def _():
        mixed(HALF, mix_recv.at[0]).wait_send()

    pair_edge.wait_recv()
    copy_to(
        o.at[pl.ds(0, 4)], edge, back_send.at[0], back_recv.at[1], partner
    ).wait_recv()

    @pl.loop(0, 4)
    def _(e):
        row = HALF * other + e + 28 * (e // 2)
        left = jnp.concatenate([w_edge[2 * e], w_edge[2 * e + 1]], axis=0)
        right = jnp.concatenate(
            [x[2 + row + offsets[0, row]], x[2 + row + offsets[1, row]]], axis=0
        )
        out[row] = (edge[e].astype(jnp.float32) + dot(left, right, 0)).astype(jnp.bfloat16)

    copy_to(
        o, out.at[pl.ds(0, HALF)], back_send.at[0], back_recv.at[0], partner
    ).wait_send()
    copy_to(
        o.at[pl.ds(0, 28)], out.at[pl.ds(0, 28)], back_send.at[0], back_recv.at[0], partner
    ).wait_recv()


def on_device(
    rhs, source_basis, target_basis, near_blocks, near_offsets,
    source_values, source_scales, target_values, target_scales,
):
    boxes = source_basis.shape[0]
    anywhere = pl.BlockSpec(memory_space=pltpu.HBM)
    bf16, f32 = jnp.bfloat16, jnp.float32
    product = pl.pallas_call(
        kernel,
        out_shape=pltpu.VMEM((boxes, ROWS, COLS), bf16),
        in_specs=[anywhere] * 9,
        out_specs=pl.BlockSpec(memory_space=pltpu.VMEM),
        scratch_shapes=[
            pltpu.VMEM((2 * HALF + 4, ROWS, COLS), bf16),
            pltpu.VMEM((HALF, ROWS, COLS), bf16),
            pltpu.VMEM((HALF, 128, 128), bf16),
            pltpu.VMEM((HALF, 128, 128), bf16),
            pltpu.VMEM((2 * HALF, 128, 128), bf16),
            pltpu.VMEM((8, 128, 128), bf16),
            pltpu.VMEM((LEVELS, 2 * HALF, 128, 128), bf16),
            pltpu.VMEM((LEVELS, 2 * HALF, 128, 128), bf16),
            pltpu.VMEM((LEVELS, HALF // 2, 2, 2, 128), f32),
            pltpu.VMEM((LEVELS, HALF // 2, 2, 2, 128), f32),
            pltpu.VMEM((HALF, 2, 128, COLS), bf16),
            pltpu.VMEM((HALF, 2, 128, COLS), bf16),
            pltpu.VMEM((HALF, ROWS, COLS), bf16),
            pltpu.VMEM((4, ROWS, COLS), bf16),
            pltpu.SMEM((2, 2 * HALF), jnp.int32),
            pltpu.SemaphoreType.DMA((11,)),
            pltpu.SemaphoreType.DMA((7,)),
            pltpu.SemaphoreType.DMA((9,)),
            pltpu.SemaphoreType.DMA((2,)),
            pltpu.SemaphoreType.DMA((2,)),
            pltpu.SemaphoreType.DMA((1,)),
            pltpu.SemaphoreType.DMA((STEPS,)),
            pltpu.SemaphoreType.DMA((1,)),
            pltpu.SemaphoreType.DMA((2,)),
            pltpu.SemaphoreType.REGULAR((8,)),
            pltpu.VMEM((2, 32, COLS), bf16),
            pltpu.SemaphoreType.DMA((2,)),
        ],
        compiler_params=pltpu.CompilerParams(
            collective_id=0, has_side_effects=True, vmem_limit_bytes=58 << 20
        ),
        name="butterfly",
    )(
        rhs.reshape(boxes, ROWS, COLS),
        jnp.swapaxes(source_basis, 1, 2),
        jnp.swapaxes(target_basis, 1, 2),
        jnp.swapaxes(near_blocks, 2, 3).reshape(2 * boxes, 64, 128),
        near_offsets.T,
        source_values.reshape(LEVELS, 2 * boxes, 64, 128),
        source_scales,
        target_values.reshape(LEVELS, 2 * boxes, 64, 128),
        target_scales,
    )
    return product.reshape(boxes * ROWS, COLS)


def solution(mesh):
    placed = (
        P("leaf", "rhs"),
        P("leaf", None, "rhs"),
        P("leaf", None, "rhs"),
        P("leaf", None, None, "rhs"),
        P("leaf", None),
        P(None, "leaf", None, None, "rhs", None),
        P(None, "leaf", None, None, None),
        P(None, "leaf", None, None, "rhs", None),
        P(None, "leaf", None, None, None),
    )
    return jax.shard_map(
        on_device, mesh=mesh, in_specs=placed, out_specs=P("leaf", "rhs"), check_vma=False
    )
```
